128 devices in a mesh: grp: 64 (over z, y, x), sub: 2 (over core).
Axes of the slice: x: 4, y: 4, z: 4, core: 2. Of those that a mesh axis runs over, the one named last changes fastest.
Arguments:
- potentials: bfloat16 [4096, 200, 200], P(('grp', 'sub')), may hold values from -6 to 6
- dimers: int32 [16384, 2], P(('grp', 'sub')), may hold values from 0 to 4095, as said below
- coupling: float32 [16384], P(('grp', 'sub')), may hold values from 0.3 to 1.5
- transform: bfloat16 [400, 400], replicated, may hold values from -0.3125 to 0.3125
Outputs:
- energies: float32 [16384, 400], P(('grp', 'sub'))
- checksum: float32 [1], replicated
The draws below stay inside these ranges and needn't reach their ends.
Inputs may be any that keep to these rules, and one draw needn't show every extreme that they name: `dimers`: each row names two different fragments. Rows d with d // 128 = o belong to owner o, and their second fragment f has f // 32 = o. Among the 128 first fragments of one owner's rows, at most 2 fall into the fragments of any one device (fragments f with f // 32 equal), and exactly 2 into some device's fragments.
All inputs are finite; a program needn't handle non-finite values.
Results may differ from the reference program's by a relative error of at most 0.0023.
Values may be sent and summed in bfloat16 or wider, within the bound.
A program may use at most 192 MiB of HBM per device.

```python
import math
import jax
import jax.numpy as jnp
from jax import lax

B = 200
FRAG_DEV = 32
DIM_DEV = 128
OWNERS = 128
FRAGS = 4096
DIMERS = 16384
PAIR = 400
CAP = 2


def draw_dimers(key, part):

    def one_owner(owner, owner_key):
        key_full, key_rest, key_local, key_order, key_second = jax.random.split(owner_key, 5)
        full = jax.random.randint(key_full, (), 0, OWNERS)
        rest = jax.random.permutation(key_rest, OWNERS * CAP - CAP)
        rest = rest + CAP * (rest >= full * CAP).astype(jnp.int32)
        first = full * CAP + jnp.arange(CAP, dtype=jnp.int32)
        slots = jnp.concatenate([first, rest[:DIM_DEV - CAP]])
        source = slots // CAP
        local = jax.random.randint(key_local, (DIM_DEV,), 0, FRAG_DEV)
        order = jax.random.permutation(key_order, DIM_DEV)
        leading = (source * FRAG_DEV + local)[order]
        second_local = jax.random.randint(key_second, (DIM_DEV,), 0, FRAG_DEV)
        second = owner * FRAG_DEV + second_local
        moved = owner * FRAG_DEV + (second_local + 1) % FRAG_DEV
        second = jnp.where(leading == second, moved, second)
        return jnp.stack([leading, second], axis=1)
    owner_keys = jax.random.split(jax.random.fold_in(key, 7), OWNERS)
    owner_ids = jnp.arange(OWNERS, dtype=jnp.int32)
    return jax.vmap(one_owner)(owner_ids, owner_keys).reshape(DIMERS, 2).astype(jnp.int32)


def shard_levels(own_key, dims, shards, least, top_value):
    gain = 1.0
    for axis_at, shards_of in shards:
        steps = jax.random.uniform(jax.random.fold_in(jax.random.fold_in(own_key, 6), axis_at), (shards_of,), jnp.float32, least / len(shards), top_value / len(shards))
        gain = gain * jnp.repeat(jnp.exp(steps), dims[axis_at] // shards_of).reshape((-1,) + (1,) * (len(dims) - 1 - axis_at))
    return gain


def normal_values(rng, shape, scale, most, cuts=(), held_as=jnp.bfloat16):
    entries = scale * jax.random.normal(rng, shape, jnp.float32)
    if cuts:
        entries = entries * shard_levels(rng, shape, cuts, -0.22, 0.18)
    return jnp.clip(entries, -most, most).astype(held_as)


def setup_inputs(seed: int = 0) -> dict:
    seeds = jax.random.split(jax.random.key(seed), 5)
    return {
        "potentials": normal_values(seeds[0], (FRAGS, B, B), 1.0, 6.0, ((0, 128),)),
        "dimers": draw_dimers(jax.random.fold_in(seeds[4], 71), 0),
        "coupling": jnp.clip(jnp.exp(math.log(1.5) - 1.60943787 * jax.random.uniform(seeds[2], (DIMERS,), jnp.float32) ** shard_levels(seeds[2], (DIMERS,), ((0, 128),), -0.2, 0.2)), 0.3, 1.5),
        "transform": normal_values(seeds[3], (PAIR, PAIR), PAIR ** -0.5, 0.3125),
    }


def block_energies(left, right, scale, transform):
    upper = transform[:B].astype(jnp.float32)
    lower = transform[B:].astype(jnp.float32)
    left_f = left.astype(jnp.float32)
    right_f = right.astype(jnp.float32)
    cross = jnp.einsum('nab,nbc->nac', left_f, right_f)
    block = (cross * (scale[:, None, None] / jnp.sqrt(jnp.float32(B)))).astype(jnp.bfloat16).astype(jnp.float32)
    top = jnp.einsum('nab,bk->nak', left_f, upper) + jnp.einsum('nab,bk->nak', block, lower)
    bottom = jnp.einsum('nab,ak->nbk', block, upper) + jnp.einsum('nab,bk->nak', right_f, lower)
    return lax.optimization_barrier(jnp.sum(upper[None] * top, axis=1)) + lax.optimization_barrier(jnp.sum(lower[None] * bottom, axis=1))

def reference(potentials, dimers, coupling, transform):
    width = 8 if DIMERS % 8 == 0 else DIMERS
    pairs = dimers.reshape(DIMERS // width, width, 2)
    scales = coupling.reshape(DIMERS // width, width)

    def one_block(item):
        pair, scale = item
        left = jnp.take(potentials, pair[:, 0], axis=0)
        right = jnp.take(potentials, pair[:, 1], axis=0)
        return block_energies(left, right, scale, transform)
    energies = lax.map(one_block, (pairs, scales)).reshape(DIMERS, 2 * B)
    weights = (jnp.arange(DIMERS).astype(jnp.float32) + 1.0) / DIMERS
    checksum = 2.0 / DIMERS * jnp.sum(weights * lax.optimization_barrier(jnp.mean(energies * energies, axis=1)))
    return (energies, checksum.reshape(1))
```

```python
import functools
import math
import jax, jax.numpy as jnp
from jax import lax
from jax.experimental import pallas as pl
from jax.experimental.pallas import tpu as pltpu
from jax.sharding import Mesh
from jax.sharding import PartitionSpec as P

MESH = pl.DeviceIdType.MESH
ROWS = 2544
HALF = 1280
NCOPY = 56

def route_kernel(lq, rq, lg, rg, rel_l, rel_r, bounce, send, recv, loc):
    z, y, x, c = (lax.axis_index(n) for n in ("grp_0", "grp_1", "grp_2", "sub"))

    def dev(dz=0, dy=0, dx=0, dc=0):
        return (lax.rem(z + dz, 4), lax.rem(y + dy, 4), lax.rem(x + dx, 4), lax.rem(c + dc, 2))

    barrier = pltpu.get_barrier_semaphore()
    partners = [dev(dx=1), dev(dx=3), dev(dy=1), dev(dy=3), dev(dz=1), dev(dz=3), dev(dc=1)]
    for p in partners:
        pl.semaphore_signal(barrier, inc=1, device_id=p, device_id_type=MESH)
    pl.semaphore_wait(barrier, len(partners))

    copies = {}

    def send_to(name, src, dst, to):
        i = len(copies)
        copy = pltpu.make_async_remote_copy(
            src_ref=src, dst_ref=dst, send_sem=send.at[i], recv_sem=recv.at[i],
            device_id=to, device_id_type=MESH)
        copy.start()
        copies[name] = copy

    got = lambda *names: [copies[n].wait_recv() for n in names]
    part = lambda d: lax.rem(x + d, 4)
    lo, hi = pl.ds(0, HALF), pl.ds(HALF, ROWS - HALF)

    def ring(dx):
        l_src = lq.at[x] if dx == 0 else lg.at[0, dx]
        r_src = rq.at[x] if dx == 0 else rg.at[0, 0, dx]
        send_to(("z+", dx), l_src, lg.at[3, dx], dev(dz=1))
        send_to(("z-", dx), l_src, lg.at[1, dx], dev(dz=3))
        send_to(("y+", dx), r_src, rg.at[0, 3, dx], dev(dy=1))
        send_to(("y-", dx), r_src, rg.at[0, 1, dx], dev(dy=3))
        send_to(("c", 0, dx), r_src, rg.at[1, 0, dx], dev(dc=1))

    def relay(dx):
        got(("z+", dx))
        send_to(("zr+", dx), lg.at[3, dx, lo], lg.at[2, dx, lo], dev(dz=1))
        got(("z-", dx))
        send_to(("zr-", dx), lg.at[1, dx, hi], lg.at[2, dx, hi], dev(dz=3))
        got(("y+", dx))
        send_to(("yr+", dx), rg.at[0, 3, dx, lo], rg.at[0, 2, dx, lo], dev(dy=1))
        send_to(("c", 3, dx), rg.at[0, 3, dx], rg.at[1, 3, dx], dev(dc=1))
        got(("y-", dx))
        send_to(("yr-", dx), rg.at[0, 1, dx, hi], rg.at[0, 2, dx, hi], dev(dy=3))
        send_to(("c", 1, dx), rg.at[0, 1, dx], rg.at[1, 1, dx], dev(dc=1))

    def last(dx):
        got(("yr+", dx), ("yr-", dx))
        send_to(("c", 2, dx), rg.at[0, 2, dx], rg.at[1, 2, dx], dev(dc=1))
        got(("zr+", dx), ("zr-", dx))

    send_to(("xl", 3), lq.at[part(1)], lg.at[0, 3], dev(dx=1))
    send_to(("xr", 1), rq.at[part(3)], rg.at[0, 0, 1], dev(dx=3))
    ring(0)
    send_to(("xr", 3), rq.at[part(1)], rg.at[0, 0, 3], dev(dx=1))
    send_to(("xl", 1), lq.at[part(3)], lg.at[0, 1], dev(dx=3))
    send_to("l_rel", lq.at[part(2)], rel_l, dev(dx=1))
    send_to("r_rel", rq.at[part(2)], rel_r, dev(dx=3))
    own = [(lq, lg.at[0, 0]), (rq, rg.at[0, 0, 0])]
    for k, (src, dst) in enumerate(own):
        into = pltpu.make_async_copy(src.at[x], bounce.at[k], loc.at[k])
        into.start()
        into.wait()
        out = pltpu.make_async_copy(bounce.at[k], dst, loc.at[2 + k])
        out.start()
        own[k] = out
    relay(0)
    got(("xl", 3), ("xr", 3))
    ring(3)
    got(("xl", 1), ("xr", 1))
    ring(1)
    got("l_rel")
    send_to(("xl", 2), rel_l, lg.at[0, 2], dev(dx=1))
    got("r_rel")
    send_to(("xr", 2), rel_r, rg.at[0, 0, 2], dev(dx=3))
    last(0)
    relay(3)
    got(("xl", 2), ("xr", 2))
    ring(2)
    relay(1)
    last(3)
    last(1)
    relay(2)
    last(2)
    for dx in range(4):
        for dy in range(4):
            copies[("c", dy, dx)].wait_recv()
    for out in own:
        out.wait()
    for copy in copies.values():
        copy.wait_send()
    assert len(copies) == NCOPY


def route(lq, rq):
    blk = (ROWS, 128)
    any_ = pl.BlockSpec(memory_space=pl.ANY)
    bf = jnp.bfloat16
    return pl.pallas_call(
        route_kernel,
        out_shape=(jax.ShapeDtypeStruct((4, 4) + blk, bf), jax.ShapeDtypeStruct((2, 4, 4) + blk, bf),
                   jax.ShapeDtypeStruct(blk, bf), jax.ShapeDtypeStruct(blk, bf)),
        in_specs=[any_, any_],
        out_specs=(any_, any_, any_, any_),
        scratch_shapes=[pltpu.VMEM((2,) + blk, bf), pltpu.SemaphoreType.DMA((NCOPY,)),
                        pltpu.SemaphoreType.DMA((NCOPY,)), pltpu.SemaphoreType.DMA((4,))],
        compiler_params=pltpu.CompilerParams(collective_id=0, has_side_effects=True, vmem_limit_bytes=60 << 20),
        name="route",
    )(lq, rq)[:2]


AXES = ("grp_0", "grp_1", "grp_2", "sub")
K = 512
MAIN, PAIRED, TAIL, REM, TABLE = 0, 1536, 2304, 2400, 2528
PROWS = 1600


def pack(m, table):
    bf = jnp.bfloat16
    main = m[:, :192].reshape(16, 2, 4, 48, 200)
    x1 = main[..., :128].transpose(2, 1, 0, 3, 4).reshape(4, 1536, 128)
    x2 = main[..., 128:192].transpose(2, 0, 3, 1, 4).reshape(4, 768, 128)
    x3 = main[..., 192:].reshape(2, 8, 2, 4, 48, 8)
    x3 = x3[:, :, ::-1].transpose(3, 0, 4, 2, 1, 5).reshape(4, 96, 128)
    rem = jnp.pad(m[:, 192:], ((0, 0), (0, 0), (0, 56))).reshape(32, 4, 2, 2, 128)
    rem = rem.transpose(1, 3, 0, 2, 4).reshape(4, 128, 128)
    table = jnp.broadcast_to(table[None], (4, 16, 128))
    return jnp.concatenate([x1, x2, x3, rem, table], axis=1).astype(bf)


def slot_table(dimers, coupling):
    source = dimers[:, 0] // 32
    same = (source[:, None] == source[None, :]).astype(jnp.int32)
    count = source.shape[0]
    before = jnp.arange(count)[None, :] < jnp.arange(count)[:, None]
    rank = jnp.sum(jnp.where(before, same, 0), axis=1)
    scale = coupling * jnp.float32(2.0 / math.sqrt(200.0))
    hi = lax.reduce_precision(scale, 8, 7)
    mid = lax.reduce_precision(scale - hi, 8, 7)
    low = scale - hi - mid
    li = (dimers[:, 0] % 32).astype(jnp.float32)
    lj = (dimers[:, 1] % 32).astype(jnp.float32)
    one = jnp.ones_like(scale)
    zero = jnp.zeros_like(scale)
    fields = jnp.stack([li, lj, hi, mid, low, one, zero, zero]).astype(jnp.bfloat16)
    hot = source[:, None] == jnp.arange(128)[None, :]
    picks = jnp.stack([hot & (rank == 0)[:, None], hot & (rank == 1)[:, None]], axis=1)
    picks = picks.reshape(count, 256).astype(jnp.bfloat16)
    table = jnp.dot(fields, picks, preferred_element_type=jnp.float32)
    return table.astype(jnp.bfloat16).reshape(16, 128), source, rank


def weights(u):
    u = jnp.pad(u, ((0, 0), (0, K - 400)))
    a, b, t = u[:128], u[128:192], jnp.tile(u[192:], (8, 1))
    return jnp.stack([
        jnp.concatenate([a, b, t]),
        jnp.concatenate([a, t, b]),
        jnp.pad(u, ((0, 56), (0, 0))),
    ])


def meet_kernel(pos, slots, scales, l_ref, r_ref, u_ref, w_ref, um_ref, ur_ref, out_ref, p_ref, q_ref, dl_ref, lhs_ref):
    step = pl.program_id(0)

    def product(src, weight, store):
        lane = lax.broadcasted_iota(jnp.int32, (48, 128), 1)
        for e in range(2):
            own = (lane < 64) if e == 0 else (lane >= 64)
            lhs_ref[e * 768:(e + 1) * 768, :128] = src[e * 768:(e + 1) * 768, :]
            for p in range(16):
                tail = (lane // 8) == (p % 8 + (8 if e == 0 else 0))
                x2 = src[PAIRED + 48 * p:PAIRED + 48 * p + 48, :]
                x3 = src[TAIL + 48 * (p // 8):TAIL + 48 * (p // 8) + 48, :]
                second = jnp.where(own, x2, jnp.where(tail, x3, jnp.zeros_like(x3)))
                at = e * 768 + 48 * p
                lhs_ref[at:at + 48, 128:] = second
        for h in range(2):
            lhs_ref[1536:1600, 128 * h:128 * h + 128] = src[REM + 64 * h:REM + 64 * h + 64, :]
        for e in range(2):
            @pl.loop(0, 3)
            def _(t):
                rows = pl.ds(pl.multiple_of(e * 768 + 256 * t, 256), 256)
                store(rows, jnp.dot(lhs_ref[rows, :], weight[e], preferred_element_type=jnp.float32))
        rows = pl.ds(1536, 64)
        store(rows, jnp.dot(lhs_ref[rows, :], weight[2], preferred_element_type=jnp.float32))

    @pl.when(step < 16)
    def _():
        def store(rows, value):
            p_ref[step, rows, :] = value

        product(l_ref.at[0], u_ref, store)

        @pl.loop(0, 32)
        def _(f):
            at = pl.multiple_of((f & 1) * 768 + (f >> 1) * 48, 8)
            prod = p_ref[step, pl.ds(at, 48), :] * um_ref[...]
            total = jnp.sum(prod, axis=0, keepdims=True)
            for r in range(2):
                total += p_ref[step, pl.ds(1536 + 2 * f + r, 1), :] * ur_ref[r:r + 1, :]
            dl_ref[pl.ds(step * 32 + f, 1), :] = total

    @pl.when(step >= 16)
    def _():
        o = step - 16

        def store(rows, value):
            q_ref[rows, :] = value

        product(r_ref.at[0], w_ref, store)

        @pl.loop(0, 32)
        def _(n):
            word = slots[o * 32 + n]

            @pl.when(word >= 1024)
            def _():
                li, lj = word & 31, (word >> 5) & 31
                s = (((n >> 3) - pos[0]) & 3) * 4 + (((n >> 1) & 3) - pos[1] & 3)
                pi = pl.multiple_of((li & 1) * 768 + (li >> 1) * 48, 8)
                qj = pl.multiple_of((lj & 1) * 768 + (lj >> 1) * 48, 8)
                prod = p_ref[s, pl.ds(pi, 48), :] * q_ref[pl.ds(qj, 48), :]
                total = jnp.sum(prod, axis=0, keepdims=True)
                for r in range(2):
                    total += p_ref[s, pl.ds(1536 + 2 * li + r, 1), :] * q_ref[pl.ds(1536 + 2 * lj + r, 1), :]
                out_ref[0, pl.ds(n, 1), :] = total * scales[o * 32 + n] + dl_ref[pl.ds(s * 32 + li, 1), :]


def meet(pos, slots, scales, lg, rg, u, w, um, ur):
    blk = (1, ROWS, 128)
    whole = lambda a: pl.BlockSpec(a.shape, lambda i, *_: (0,) * a.ndim, pipeline_mode=pl.Buffered(1))
    return pl.pallas_call(
        meet_kernel,
        out_shape=jax.ShapeDtypeStruct((32, 32, K), jnp.float32),
        grid_spec=pltpu.PrefetchScalarGridSpec(
            num_scalar_prefetch=3, grid=(48,),
            in_specs=[
                pl.BlockSpec(blk, lambda i, *_: (jnp.minimum(i, 15), 0, 0)),
                pl.BlockSpec(blk, lambda i, *_: (jnp.maximum(i - 16, 0), 0, 0)),
                whole(u), whole(w), whole(um), whole(ur),
            ],
            out_specs=pl.BlockSpec((1, 32, K), lambda i, *_: (jnp.maximum(i - 16, 0), 0, 0)),
            scratch_shapes=[
                pltpu.VMEM((16, PROWS, K), jnp.float32), pltpu.VMEM((PROWS, K), jnp.float32),
                pltpu.VMEM((512, K), jnp.float32), pltpu.VMEM((PROWS, 256), jnp.bfloat16),
            ],
        ),
        compiler_params=pltpu.CompilerParams(dimension_semantics=("arbitrary",), vmem_limit_bytes=67043328),
        name="meet",
    )(pos, slots, scales, lg.reshape(16, ROWS, 128), rg.reshape(32, ROWS, 128), u, w, um, ur)


def finish_kernel(where, parts, dr_ref, en_ref, sum_ref, got_ref, part_ref, inbox_ref, send, recv, loc):
    z, y, x, c = (lax.axis_index(n) for n in AXES)

    def dev(dz=0, dy=0, dx=0, dc=0):
        return (lax.rem(z + dz, 4), lax.rem(y + dy, 4), lax.rem(x + dx, 4), lax.rem(c + dc, 2))

    barrier = pltpu.get_barrier_semaphore()
    plane = [(dc, dy, dx) for dx in (2, 1, 3, 0) for dy in (2, 1, 3, 0) for dc in (1, 0)][:-1]
    partners = [dev(dc=dc, dy=dy, dx=dx) for dc, dy, dx in plane] + [dev(dz=d) for d in (1, 2, 3)]
    for p in partners:
        pl.semaphore_signal(barrier, inc=1, device_id=p, device_id_type=MESH)
    pl.semaphore_wait(barrier, len(partners))
    copies = []

    def send_to(src, dst, to):
        i = len(copies)
        copy = pltpu.make_async_remote_copy(
            src_ref=src, dst_ref=dst, send_sem=send.at[i], recv_sem=recv.at[i],
            device_id=to, device_id_type=MESH)
        copy.start()
        copies.append(copy)
        return copy

    for dc, dy, dx in plane:
        send_to(parts.at[dc, dy, dx], got_ref.at[dc, (4 - dy) % 4, (4 - dx) % 4], dev(dc=dc, dy=dy, dx=dx))
    own = pltpu.make_async_copy(parts.at[0, 0, 0], got_ref.at[0, 0, 0], loc.at[0])
    own.start()
    own.wait()
    for copy in copies:
        copy.wait_recv()

    me = ((z * 4 + y) * 4 + x) * 2 + c

    @pl.loop(0, 128)
    def _(d):
        dc, dy, n, lj = where[0, d], where[1, d], where[2, d], where[3, d]
        row = dr_ref[pl.ds(lj, 1), :]
        for dx in range(4):
            row += got_ref[dc, dy, dx, pl.ds(n, 1), :]
        en_ref[pl.ds(d, 1), :] = row[:, :400]

    value = en_ref[...]
    mean = jnp.sum(value * value, axis=1, keepdims=True) * jnp.float32(1.0 / 400.0)
    index = (me * 128 + lax.broadcasted_iota(jnp.int32, (128, 1), 0)).astype(jnp.float32)
    total = jnp.sum((index + 1.0) * jnp.float32(1.0 / 16384.0) * mean, axis=0, keepdims=True)
    total = jnp.broadcast_to(total * jnp.float32(2.0 / 16384.0), (8, 128))
    stages = [[dict(dx=d) for d in (1, 2, 3)], [dict(dy=d) for d in (1, 2, 3)], [dict(dz=d) for d in (1, 2, 3)], [dict(dc=1)]]
    slot = 0
    for k, stage in enumerate(stages):
        part_ref[k] = total
        sent = []
        for j, to in enumerate(stage):
            sent.append((slot, send_to(part_ref.at[k], inbox_ref.at[slot], dev(**to))))
            slot += 1
        for at, copy in sent:
            copy.wait_recv()
        values = [total] + [inbox_ref[at] for at, _ in sent]
        if len(values) == 4:
            total = (values[0] + values[2]) + (values[1] + values[3])
        else:
            total = values[0] + values[1]
    sum_ref[...] = total
    for copy in copies:
        copy.wait_send()


def finish(where, parts, dr):
    n = 41
    vmem = pl.BlockSpec(memory_space=pltpu.VMEM)
    return pl.pallas_call(
        finish_kernel,
        out_shape=(jax.ShapeDtypeStruct((128, 400), jnp.float32), jax.ShapeDtypeStruct((8, 128), jnp.float32)),
        in_specs=[pl.BlockSpec(memory_space=pltpu.SMEM), pl.BlockSpec(memory_space=pl.ANY), vmem],
        out_specs=(vmem, vmem),
        scratch_shapes=[
            pltpu.VMEM((2, 4, 4, 32, K), jnp.float32), pltpu.VMEM((4, 8, 128), jnp.float32),
            pltpu.VMEM((10, 8, 128), jnp.float32), pltpu.SemaphoreType.DMA((n,)),
            pltpu.SemaphoreType.DMA((n,)), pltpu.SemaphoreType.DMA((1,)),
        ],
        compiler_params=pltpu.CompilerParams(collective_id=1, has_side_effects=True, vmem_limit_bytes=32 << 20),
        name="finish",
    )(where, parts.reshape(2, 4, 4, 32, K), dr)


def local(potentials, dimers, coupling, transform):
    z, y, x, c = (lax.axis_index(n) for n in AXES)
    upper, lower = transform[:200], transform[200:]
    table, source, rank = slot_table(dimers, coupling)
    lq = pack(potentials.transpose(0, 2, 1), jnp.zeros_like(table))
    rq = pack(potentials, table)
    lg, rg = route(lq, rq)

    tab = rg[:, :, :, TABLE:, :].reshape(32, 8, 2, 4, 4, 4, 2)
    tab = lax.dynamic_index_in_dim(tab, y, 4, keepdims=False)
    tab = lax.dynamic_index_in_dim(tab, c, 5, keepdims=False)
    tab = tab.transpose(1, 0, 3, 4, 2).reshape(8, 1024).astype(jnp.float32)
    slots = (tab[0] + 32.0 * tab[1] + 1024.0 * tab[5]).astype(jnp.int32)
    scales = tab[2] + tab[3] + tab[4]

    pad = ((0, 0), (0, K - 400))
    up = jnp.pad(upper, pad).astype(jnp.float32)
    um = lax.dynamic_slice_in_dim(up, 48 * x, 48, 0)
    ur = lax.dynamic_slice_in_dim(up, 192 + 2 * x, 2, 0)
    pos = jnp.stack([z, x])
    parts = meet(pos, slots, scales, lg, rg, weights(upper), weights(lower), um, ur)

    own = jnp.einsum("fab,bk->fak", potentials, lower, preferred_element_type=jnp.float32)
    dr = jnp.pad(jnp.sum(own * lower.astype(jnp.float32)[None], axis=1), pad)
    zs, ys, xs, cs = source // 32, (source // 8) % 4, (source // 2) % 4, source % 2
    where = jnp.stack([(cs - c) % 2, (ys - y) % 4, (zs * 4 + xs) * 2 + rank, dimers[:, 1] % 32])
    energies, total = finish(where, parts, dr)
    return energies, total[0, :1]


def solution(mesh):
    split = Mesh(mesh.devices.reshape(4, 4, 4, mesh.shape["sub"]), AXES)
    return jax.shard_map(
        local,
        mesh=split,
        in_specs=(P(AXES, None, None), P(AXES, None), P(AXES), P()),
        out_specs=(P(AXES, None), P()),
        check_vma=False,
    )
```

```python
import functools
import math
import jax, jax.numpy as jnp
from jax import lax
from jax.experimental import pallas as pl
from jax.experimental.pallas import tpu as pltpu
from jax.sharding import Mesh
from jax.sharding import PartitionSpec as P

MESH = pl.DeviceIdType.MESH
ROWS = 2544
HALF = 1280
NCOPY = 56

def route_kernel(lq, rq, lg, rg, rel_l, rel_r, bounce, send, recv, loc):
    z, y, x, c = (lax.axis_index(n) for n in ("grp_0", "grp_1", "grp_2", "sub"))

    def dev(dz=0, dy=0, dx=0, dc=0):
        return (lax.rem(z + dz, 4), lax.rem(y + dy, 4), lax.rem(x + dx, 4), lax.rem(c + dc, 2))

    barrier = pltpu.get_barrier_semaphore()
    partners = [dev(dx=1), dev(dx=3), dev(dy=1), dev(dy=3), dev(dz=1), dev(dz=3), dev(dc=1)]
    for p in partners:
        pl.semaphore_signal(barrier, inc=1, device_id=p, device_id_type=MESH)
    pl.semaphore_wait(barrier, len(partners))

    copies = {}

    def send_to(name, src, dst, to):
        i = len(copies)
        copy = pltpu.make_async_remote_copy(
            src_ref=src, dst_ref=dst, send_sem=send.at[i], recv_sem=recv.at[i],
            device_id=to, device_id_type=MESH)
        copy.start()
        copies[name] = copy

    got = lambda *names: [copies[n].wait_recv() for n in names]
    part = lambda d: lax.rem(x + d, 4)
    lo, hi = pl.ds(0, HALF), pl.ds(HALF, ROWS - HALF)

    def ring(dx):
        l_src = lq.at[x] if dx == 0 else lg.at[0, dx]
        r_src = rq.at[x] if dx == 0 else rg.at[0, 0, dx]
        send_to(("z+", dx), l_src, lg.at[3, dx], dev(dz=1))
        send_to(("z-", dx), l_src, lg.at[1, dx], dev(dz=3))
        send_to(("y+", dx), r_src, rg.at[0, 3, dx], dev(dy=1))
        send_to(("y-", dx), r_src, rg.at[0, 1, dx], dev(dy=3))
        send_to(("c", 0, dx), r_src, rg.at[1, 0, dx], dev(dc=1))

    def relay(dx):
        got(("z+", dx))
        send_to(("zr+", dx), lg.at[3, dx, lo], lg.at[2, dx, lo], dev(dz=1))
        got(("z-", dx))
        send_to(("zr-", dx), lg.at[1, dx, hi], lg.at[2, dx, hi], dev(dz=3))
        got(("y+", dx))
        send_to(("yr+", dx), rg.at[0, 3, dx, lo], rg.at[0, 2, dx, lo], dev(dy=1))
        send_to(("c", 3, dx), rg.at[0, 3, dx], rg.at[1, 3, dx], dev(dc=1))
        got(("y-", dx))
        send_to(("yr-", dx), rg.at[0, 1, dx, hi], rg.at[0, 2, dx, hi], dev(dy=3))
        send_to(("c", 1, dx), rg.at[0, 1, dx], rg.at[1, 1, dx], dev(dc=1))

    def last(dx):
        got(("yr+", dx), ("yr-", dx))
        send_to(("c", 2, dx), rg.at[0, 2, dx], rg.at[1, 2, dx], dev(dc=1))
        got(("zr+", dx), ("zr-", dx))

    send_to(("xl", 3), lq.at[part(1)], lg.at[0, 3], dev(dx=1))
    send_to(("xr", 1), rq.at[part(3)], rg.at[0, 0, 1], dev(dx=3))
    ring(0)
    send_to(("xr", 3), rq.at[part(1)], rg.at[0, 0, 3], dev(dx=1))
    send_to(("xl", 1), lq.at[part(3)], lg.at[0, 1], dev(dx=3))
    send_to("l_rel", lq.at[part(2)], rel_l, dev(dx=1))
    send_to("r_rel", rq.at[part(2)], rel_r, dev(dx=3))
    own = [(lq, lg.at[0, 0]), (rq, rg.at[0, 0, 0])]
    for k, (src, dst) in enumerate(own):
        into = pltpu.make_async_copy(src.at[x], bounce.at[k], loc.at[k])
        into.start()
        into.wait()
        out = pltpu.make_async_copy(bounce.at[k], dst, loc.at[2 + k])
        out.start()
        own[k] = out
    relay(0)
    got(("xl", 3), ("xr", 3))
    ring(3)
    got(("xl", 1), ("xr", 1))
    ring(1)
    got("l_rel")
    send_to(("xl", 2), rel_l, lg.at[0, 2], dev(dx=1))
    got("r_rel")
    send_to(("xr", 2), rel_r, rg.at[0, 0, 2], dev(dx=3))
    last(0)
    relay(3)
    got(("xl", 2), ("xr", 2))
    ring(2)
    relay(1)
    last(3)
    last(1)
    relay(2)
    last(2)
    for dx in range(4):
        for dy in range(4):
            copies[("c", dy, dx)].wait_recv()
    for out in own:
        out.wait()
    for copy in copies.values():
        copy.wait_send()
    assert len(copies) == NCOPY


def route(lq, rq):
    blk = (ROWS, 128)
    any_ = pl.BlockSpec(memory_space=pl.ANY)
    bf = jnp.bfloat16
    return pl.pallas_call(
        route_kernel,
        out_shape=(jax.ShapeDtypeStruct((4, 4) + blk, bf), jax.ShapeDtypeStruct((2, 4, 4) + blk, bf),
                   jax.ShapeDtypeStruct(blk, bf), jax.ShapeDtypeStruct(blk, bf)),
        in_specs=[any_, any_],
        out_specs=(any_, any_, any_, any_),
        scratch_shapes=[pltpu.VMEM((2,) + blk, bf), pltpu.SemaphoreType.DMA((NCOPY,)),
                        pltpu.SemaphoreType.DMA((NCOPY,)), pltpu.SemaphoreType.DMA((4,))],
        compiler_params=pltpu.CompilerParams(collective_id=0, has_side_effects=True, vmem_limit_bytes=60 << 20),
        name="route",
    )(lq, rq)[:2]


AXES = ("grp_0", "grp_1", "grp_2", "sub")
K = 512
MAIN, PAIRED, TAIL, REM, TABLE = 0, 1536, 2304, 2400, 2528
PROWS = 1600


def pack_kernel(pot_ref, perm_ref, tab_ref, lq_ref, rq_ref, wide_ref, rem_ref):
    lane = lax.broadcasted_iota(jnp.int32, (192, 128), 1)
    zero = jnp.zeros((192, 128), jnp.float32)
    wide_ref[...] = jnp.zeros_like(wide_ref)
    outs = (lq_ref, rq_ref)

    def pair(g, p, tails):
        new = []
        for side in range(2):
            out = outs[side]
            for e in range(2):
                f = 16 * g + 2 * p + e
                m = pot_ref[f].astype(jnp.float32)
                if side == 0:
                    m = m.T
                wide_ref[side, e, :, :200] = m
                rem_ref[side, pl.ds(pl.multiple_of(8 * f, 8), 8), :] = wide_ref[side, e, 192:200, :]
                for q in range(4):
                    at = pl.multiple_of(e * 768 + 48 * (8 * g + p), 16)
                    out[q, pl.ds(at, 48), :] = m[48 * q:48 * q + 48, :128].astype(jnp.bfloat16)
            s0 = wide_ref[side, 0, :192, 128:]
            s1 = wide_ref[side, 1, :192, 128:]
            x2 = jnp.where(lane < 64, s0, pltpu.roll(s1, 64, 1)).astype(jnp.bfloat16)
            for q in range(4):
                at = pl.multiple_of(PAIRED + 48 * (8 * g + p), 16)
                out[q, pl.ds(at, 48), :] = x2[48 * q:48 * q + 48]
            block = lane // 8
            tail = jnp.where(block == 8 + p, pltpu.roll(s0, 8 * p, 1), tails[side])
            new.append(jnp.where(block == p, pltpu.roll(s1, 64 + 8 * p, 1), tail))
        return tuple(new)

    for g in range(2):
        tails = lax.fori_loop(0, 8, functools.partial(pair, g), (zero, zero))
        for side in range(2):
            tail = tails[side].astype(jnp.bfloat16)
            for q in range(4):
                outs[side][q, TAIL + 48 * g:TAIL + 48 * g + 48, :] = tail[48 * q:48 * q + 48]
    for side in range(2):
        rem = jnp.dot(perm_ref[...], rem_ref[side].astype(jnp.bfloat16), preferred_element_type=jnp.float32)
        for q in range(4):
            for h in range(2):
                at = REM + 64 * h
                outs[side][q, at:at + 64, :] = rem[64 * q:64 * q + 64, 128 * h:128 * h + 128].astype(jnp.bfloat16)
            outs[side][q, TABLE:, :] = tab_ref[...]


def pack(potentials, table):
    row = jnp.arange(256)
    q, f, r = row // 64, (row % 64) // 2, row % 2
    perm = ((f * 8 + 2 * q + r)[:, None] == row[None, :]).astype(jnp.bfloat16)
    vmem = pl.BlockSpec(memory_space=pltpu.VMEM)
    shape = jax.ShapeDtypeStruct((4, ROWS, 128), jnp.bfloat16)
    return pl.pallas_call(
        pack_kernel,
        out_shape=(shape, shape),
        in_specs=[vmem, vmem, vmem],
        out_specs=(vmem, vmem),
        scratch_shapes=[pltpu.VMEM((2, 2, 200, 256), jnp.float32), pltpu.VMEM((2, 256, 256), jnp.float32)],
        compiler_params=pltpu.CompilerParams(vmem_limit_bytes=40 << 20),
        name="pack",
    )(potentials, perm, table)


def slot_table(dimers, coupling):
    source = dimers[:, 0] // 32
    same = (source[:, None] == source[None, :]).astype(jnp.int32)
    count = source.shape[0]
    before = jnp.arange(count)[None, :] < jnp.arange(count)[:, None]
    rank = jnp.sum(jnp.where(before, same, 0), axis=1)
    scale = coupling * jnp.float32(2.0 / math.sqrt(200.0))
    hi = lax.reduce_precision(scale, 8, 7)
    mid = lax.reduce_precision(scale - hi, 8, 7)
    low = scale - hi - mid
    li = (dimers[:, 0] % 32).astype(jnp.float32)
    lj = (dimers[:, 1] % 32).astype(jnp.float32)
    one = jnp.ones_like(scale)
    zero = jnp.zeros_like(scale)
    fields = jnp.stack([li, lj, hi, mid, low, one, zero, zero]).astype(jnp.bfloat16)
    hot = source[:, None] == jnp.arange(128)[None, :]
    picks = jnp.stack([hot & (rank == 0)[:, None], hot & (rank == 1)[:, None]], axis=1)
    picks = picks.reshape(count, 256).astype(jnp.bfloat16)
    table = jnp.dot(fields, picks, preferred_element_type=jnp.float32)
    return table.astype(jnp.bfloat16).reshape(16, 128), source, rank


def weights(u):
    u = jnp.pad(u, ((0, 0), (0, K - 400)))
    a, b, t = u[:128], u[128:192], jnp.tile(u[192:], (8, 1))
    return jnp.stack([
        jnp.concatenate([a, b, t]),
        jnp.concatenate([a, t, b]),
    ])


def meet_kernel(gi_ref, gj_ref, li_ref, lj_ref, scales, l_ref, r_ref, u_ref, w_ref, um_ref, ur_ref, got_ref, p_ref, pr_ref, q_ref, qr_ref, dl_ref, lhs_ref, out_ref, send, recv, loc):
    step = pl.program_id(0)
    z, y, x, c = (lax.axis_index(n) for n in AXES)

    def dev(o):
        return (z, lax.rem(y + lax.rem(o // 4, 4), 4), lax.rem(x + lax.rem(o, 4), 4), lax.rem(c + o // 16, 2))

    def copy_of(o):
        to = (o // 16) * 16 + lax.rem(4 - lax.rem(o // 4, 4), 4) * 4 + lax.rem(4 - lax.rem(o, 4), 4)
        return pltpu.make_async_remote_copy(
            src_ref=out_ref.at[o], dst_ref=got_ref.at[to], send_sem=send.at[o], recv_sem=recv.at[o],
            device_id=dev(o), device_id_type=MESH)

    @pl.when(step == 0)
    def _():
        barrier = pltpu.get_barrier_semaphore()
        for o in range(1, 32):
            pl.semaphore_signal(barrier, inc=1, device_id=dev(jnp.int32(o)), device_id_type=MESH)
        pl.semaphore_wait(barrier, 31)

    def product(src, weight, store, rest):
        lane = lax.broadcasted_iota(jnp.int32, (48, 128), 1)
        for e in range(2):
            own = (lane < 64) if e == 0 else (lane >= 64)
            lhs_ref[e * 832:e * 832 + 768, :128] = src[e * 768:(e + 1) * 768, :]
            for p in range(16):
                tail = (lane // 8) == (p % 8 + (8 if e == 0 else 0))
                x2 = src[PAIRED + 48 * p:PAIRED + 48 * p + 48, :]
                x3 = src[TAIL + 48 * (p // 8):TAIL + 48 * (p // 8) + 48, :]
                second = jnp.where(own, x2, jnp.where(tail, x3, jnp.zeros_like(x3)))
                at = e * 832 + 48 * p
                lhs_ref[at:at + 48, 128:] = second
        for h in range(2):
            lhs_ref[768:832, 128 * h:128 * h + 128] = src[REM + 64 * h:REM + 64 * h + 64, :]
        first = jnp.dot(lhs_ref[:832, :], weight[0], preferred_element_type=jnp.float32)
        store(0, first[:768].reshape(48, 16, K))
        rest(first[768:])
        second = jnp.dot(lhs_ref[832:, :], weight[1], preferred_element_type=jnp.float32)
        store(48, second.reshape(48, 16, K))

    @pl.when(step < 16)
    def _():
        def store(at, value):
            p_ref[step, at:at + 48] = value

        def rest(value):
            pr_ref[step] = value

        product(l_ref.at[0], u_ref, store, rest)

        @pl.loop(0, 8)
        def _(t):
            for k in range(4):
                f = 4 * t + k
                group = (k % 2) * 48 + (2 * t + k // 2) * 3
                prod = p_ref[step, pl.ds(group, 3)].reshape(48, K) * um_ref[...]
                total = jnp.sum(prod, axis=0, keepdims=True)
                for r in range(2):
                    total += pr_ref[step, pl.ds(2 * f + r, 1), :] * ur_ref[r:r + 1, :]
                dl_ref[step, pl.ds(f, 1), :] = total

    @pl.when(step >= 16)
    def _():
        o = 47 - step

        def store(at, value):
            q_ref[at:at + 48] = value

        def rest(value):
            qr_ref[...] = value

        product(r_ref.at[0], w_ref, store, rest)

        @pl.loop(0, 8)
        def _(t):
            for k in range(4):
                zs, xs, r = t // 2, lax.rem(t, 2) * 2 + k // 2, k % 2
                lane = ((zs * 4 + y) * 4 + xs) * 2 + c
                row = o * 2 + r
                gi, gj, li, lj = gi_ref[row, lane], gj_ref[row, lane], li_ref[row, lane], lj_ref[row, lane]
                s = lax.rem(zs - z + 4, 4) * 4 + lax.rem(xs - x + 4, 4)
                prod = p_ref[s, pl.ds(gi, 3)] * q_ref[pl.ds(gj, 3)]
                total = jnp.sum(prod.reshape(48, K), axis=0, keepdims=True)
                for i in range(2):
                    total += pr_ref[s, pl.ds(2 * li + i, 1), :] * qr_ref[pl.ds(2 * lj + i, 1), :]
                out_ref[o, pl.ds(4 * t + k, 1), :] = total * scales[row, lane] + dl_ref[s, pl.ds(li, 1), :]

        @pl.when(o > 0)
        def _():
            copy_of(o).start()

        @pl.when(o == 0)
        def _():
            own = pltpu.make_async_copy(out_ref.at[0], got_ref.at[0], loc.at[0])
            own.start()
            own.wait()
            for k in range(1, 32):
                copy_of(jnp.int32(k)).wait_recv()
            for k in range(1, 32):
                copy_of(jnp.int32(k)).wait_send()


def meet(tables, lg, rg, u, w, um, ur):
    blk = (1, ROWS, 128)
    whole = lambda a: pl.BlockSpec(a.shape, lambda i, *_: (0,) * a.ndim, pipeline_mode=pl.Buffered(1))
    return pl.pallas_call(
        meet_kernel,
        out_shape=jax.ShapeDtypeStruct((32, 32, K), jnp.float32),
        grid_spec=pltpu.PrefetchScalarGridSpec(
            num_scalar_prefetch=5, grid=(48,),
            in_specs=[
                pl.BlockSpec(blk, lambda i, *_: (jnp.minimum(i, 15), 0, 0)),
                pl.BlockSpec(blk, lambda i, *_: (jnp.minimum(47 - i, 31), 0, 0)),
                whole(u), whole(w), whole(um), whole(ur),
            ],
            out_specs=pl.BlockSpec(memory_space=pl.ANY),
            scratch_shapes=[
                pltpu.VMEM((16, 96, 16, K), jnp.float32), pltpu.VMEM((16, 64, K), jnp.float32),
                pltpu.VMEM((96, 16, K), jnp.float32), pltpu.VMEM((64, K), jnp.float32),
                pltpu.VMEM((16, 32, K), jnp.float32), pltpu.VMEM((PROWS, 256), jnp.bfloat16),
                pltpu.VMEM((32, 32, K), jnp.float32), pltpu.SemaphoreType.DMA((32,)),
                pltpu.SemaphoreType.DMA((32,)), pltpu.SemaphoreType.DMA((1,)),
            ],
        ),
        compiler_params=pltpu.CompilerParams(dimension_semantics=("arbitrary",), vmem_limit_bytes=67043328,
                                             collective_id=2, has_side_effects=True),
        name="meet",
    )(*tables, lg.reshape(16, ROWS, 128), rg.reshape(32, ROWS, 128), u, w, um, ur)


def finish_kernel(where, got_ref, dr_ref, en_ref, sum_ref, part_ref, inbox_ref, send, recv):
    z, y, x, c = (lax.axis_index(n) for n in AXES)

    def dev(dz=0, dy=0, dx=0, dc=0):
        return (lax.rem(z + dz, 4), lax.rem(y + dy, 4), lax.rem(x + dx, 4), lax.rem(c + dc, 2))

    barrier = pltpu.get_barrier_semaphore()
    partners = [dev(**{k: d}) for k in ("dx", "dy", "dz") for d in (1, 2, 3)] + [dev(dc=1)]
    for p in partners:
        pl.semaphore_signal(barrier, inc=1, device_id=p, device_id_type=MESH)
    pl.semaphore_wait(barrier, len(partners))
    copies = []

    def send_to(src, dst, to):
        i = len(copies)
        copy = pltpu.make_async_remote_copy(
            src_ref=src, dst_ref=dst, send_sem=send.at[i], recv_sem=recv.at[i],
            device_id=to, device_id_type=MESH)
        copy.start()
        copies.append(copy)
        return copy

    me = ((z * 4 + y) * 4 + x) * 2 + c

    @pl.loop(0, 128)
    def _(d):
        dc, dy, n, lj = where[0, d], where[1, d], where[2, d], where[3, d]
        row = dr_ref[pl.ds(lj, 1), :]
        for dx in range(4):
            row += got_ref[dc, dy, dx, pl.ds(n, 1), :]
        en_ref[pl.ds(d, 1), :] = row[:, :400]

    value = en_ref[...]
    mean = jnp.sum(value * value, axis=1, keepdims=True) * jnp.float32(1.0 / 400.0)
    index = (me * 128 + lax.broadcasted_iota(jnp.int32, (128, 1), 0)).astype(jnp.float32)
    total = jnp.sum((index + 1.0) * jnp.float32(1.0 / 16384.0) * mean, axis=0, keepdims=True)
    total = jnp.broadcast_to(total * jnp.float32(2.0 / 16384.0), (8, 128))
    stages = [[dict(dx=d) for d in (1, 2, 3)], [dict(dy=d) for d in (1, 2, 3)], [dict(dz=d) for d in (1, 2, 3)], [dict(dc=1)]]
    slot = 0
    for k, stage in enumerate(stages):
        part_ref[k] = total
        sent = []
        for j, to in enumerate(stage):
            sent.append((slot, send_to(part_ref.at[k], inbox_ref.at[slot], dev(**to))))
            slot += 1
        for at, copy in sent:
            copy.wait_recv()
        values = [total] + [inbox_ref[at] for at, _ in sent]
        if len(values) == 4:
            total = (values[0] + values[2]) + (values[1] + values[3])
        else:
            total = values[0] + values[1]
    sum_ref[...] = total
    for copy in copies:
        copy.wait_send()


def finish(where, parts, dr):
    n = 10
    vmem = pl.BlockSpec(memory_space=pltpu.VMEM)
    return pl.pallas_call(
        finish_kernel,
        out_shape=(jax.ShapeDtypeStruct((128, 400), jnp.float32), jax.ShapeDtypeStruct((8, 128), jnp.float32)),
        in_specs=[pl.BlockSpec(memory_space=pltpu.SMEM), vmem, vmem],
        out_specs=(vmem, vmem),
        scratch_shapes=[
            pltpu.VMEM((4, 8, 128), jnp.float32),
            pltpu.VMEM((10, 8, 128), jnp.float32), pltpu.SemaphoreType.DMA((n,)),
            pltpu.SemaphoreType.DMA((n,)),
        ],
        compiler_params=pltpu.CompilerParams(collective_id=1, has_side_effects=True, vmem_limit_bytes=32 << 20),
        name="finish",
    )(where, parts.reshape(2, 4, 4, 32, K), dr)


def local(potentials, dimers, coupling, transform):
    z, y, x, c = (lax.axis_index(n) for n in AXES)
    upper, lower = transform[:200], transform[200:]
    table, source, rank = slot_table(dimers, coupling)
    lq, rq = pack(potentials, table)
    lg, rg = route(lq, rq)

    tab = rg[:, :, :, TABLE:, :].reshape(32, 16, 128).astype(jnp.float32)
    li, lj = tab[:, 0:2].astype(jnp.int32).reshape(64, 128), tab[:, 2:4].astype(jnp.int32).reshape(64, 128)
    scales = (tab[:, 4:6] + tab[:, 6:8] + tab[:, 8:10]).reshape(64, 128)
    tables = [(v % 2) * 48 + (v // 2) * 3 for v in (li, lj)] + [li, lj, scales]

    pad = ((0, 0), (0, K - 400))
    up = jnp.pad(upper, pad).astype(jnp.float32)
    um = lax.dynamic_slice_in_dim(up, 48 * x, 48, 0)
    ur = lax.dynamic_slice_in_dim(up, 192 + 2 * x, 2, 0)
    parts = meet(tables, lg, rg, weights(upper), weights(lower), um, ur)

    own = jnp.einsum("fab,bk->fak", potentials, lower, preferred_element_type=jnp.float32)
    dr = jnp.pad(jnp.sum(own * lower.astype(jnp.float32)[None], axis=1), pad)
    zs, ys, xs, cs = source // 32, (source // 8) % 4, (source // 2) % 4, source % 2
    where = jnp.stack([(cs - c) % 2, (ys - y) % 4, (zs * 4 + xs) * 2 + rank, dimers[:, 1] % 32])
    energies, total = finish(where, parts, dr)
    return energies, total[0, :1]


def solution(mesh):
    split = Mesh(mesh.devices.reshape(4, 4, 4, mesh.shape["sub"]), AXES)
    return jax.shard_map(
        local,
        mesh=split,
        in_specs=(P(AXES, None, None), P(AXES, None), P(AXES), P()),
        out_specs=(P(AXES, None), P()),
        check_vma=False,
    )
```

```python
import functools
import math
import jax
import jax.numpy as jnp
from jax import lax
from jax.experimental import pallas as pl
from jax.experimental.pallas import tpu as pltpu
from jax.sharding import Mesh
from jax.sharding import PartitionSpec as P

MESH = pl.DeviceIdType.MESH
AXES = ("grp_0", "grp_1", "grp_2", "sub")
K = 512
ROWS = 2528
HALF = 1280
NCOPY = 56
PAIRED, TAIL, REM = 1536, 2304, 2400
ORDER = {0: 0, 3: 1, 1: 2, 2: 3}


def pack_kernel(pot_ref, perm_ref, lq_ref, rq_ref, wide_ref, rem_ref):
    lane = lax.broadcasted_iota(jnp.int32, (192, 128), 1)
    zero = jnp.zeros((192, 128), jnp.float32)
    wide_ref[...] = jnp.zeros_like(wide_ref)
    outs = (lq_ref, rq_ref)

    def pair(g, p, tails):
        new = []
        for side in range(2):
            out = outs[side]
            for e in range(2):
                f = 16 * g + 2 * p + e
                m = pot_ref[f].astype(jnp.float32)
                if side == 0:
                    m = m.T
                wide_ref[side, e, :, :200] = m
                rem_ref[side, pl.ds(pl.multiple_of(8 * f, 8), 8), :] = wide_ref[side, e, 192:200, :]
                for q in range(4):
                    at = pl.multiple_of(e * 768 + 48 * (8 * g + p), 16)
                    out[q, pl.ds(at, 48), :] = m[48 * q:48 * q + 48, :128].astype(jnp.bfloat16)
            s0 = wide_ref[side, 0, :192, 128:]
            s1 = wide_ref[side, 1, :192, 128:]
            x2 = jnp.where(lane < 64, s0, pltpu.roll(s1, 64, 1)).astype(jnp.bfloat16)
            for q in range(4):
                at = pl.multiple_of(PAIRED + 48 * (8 * g + p), 16)
                out[q, pl.ds(at, 48), :] = x2[48 * q:48 * q + 48]
            block = lane // 8
            tail = jnp.where(block == 8 + p, pltpu.roll(s0, 8 * p, 1), tails[side])
            new.append(jnp.where(block == p, pltpu.roll(s1, 64 + 8 * p, 1), tail))
        return tuple(new)

    for g in range(2):
        tails = lax.fori_loop(0, 8, functools.partial(pair, g), (zero, zero))
        for side in range(2):
            tail = tails[side].astype(jnp.bfloat16)
            for q in range(4):
                outs[side][q, TAIL + 48 * g:TAIL + 48 * g + 48, :] = tail[48 * q:48 * q + 48]
    for side in range(2):
        rem = jnp.dot(perm_ref[...], rem_ref[side].astype(jnp.bfloat16), preferred_element_type=jnp.float32)
        for q in range(4):
            for h in range(2):
                at = REM + 64 * h
                outs[side][q, at:at + 64, :] = rem[64 * q:64 * q + 64, 128 * h:128 * h + 128].astype(jnp.bfloat16)


def pack(potentials):
    row = jnp.arange(256)
    q, f, r = row // 64, (row % 64) // 2, row % 2
    perm = ((f * 8 + 2 * q + r)[:, None] == row[None, :]).astype(jnp.bfloat16)
    vmem = pl.BlockSpec(memory_space=pltpu.VMEM)
    shape = jax.ShapeDtypeStruct((4, ROWS, 128), jnp.bfloat16)
    return pl.pallas_call(
        pack_kernel,
        out_shape=(shape, shape),
        in_specs=[vmem, vmem],
        out_specs=(vmem, vmem),
        scratch_shapes=[pltpu.VMEM((2, 2, 200, 256), jnp.float32), pltpu.VMEM((2, 256, 256), jnp.float32)],
        compiler_params=pltpu.CompilerParams(vmem_limit_bytes=40 << 20),
        name="pack",
    )(potentials, perm)


def slot_table(dimers, coupling):
    source = dimers[:, 0] // 32
    same = (source[:, None] == source[None, :]).astype(jnp.int32)
    count = source.shape[0]
    before = jnp.arange(count)[None, :] < jnp.arange(count)[:, None]
    rank = jnp.sum(jnp.where(before, same, 0), axis=1)
    scale = coupling * jnp.float32(2.0 / math.sqrt(200.0))
    hi = lax.reduce_precision(scale, 8, 7)
    mid = lax.reduce_precision(scale - hi, 8, 7)
    low = scale - hi - mid
    li = (dimers[:, 0] % 32).astype(jnp.float32)
    lj = (dimers[:, 1] % 32).astype(jnp.float32)
    zero = jnp.zeros_like(scale)
    fields = jnp.stack([li, lj, hi, mid, low, zero, zero, zero]).astype(jnp.bfloat16)
    hot = source[:, None] == jnp.arange(128)[None, :]
    picks = jnp.stack([hot & (rank == 0)[:, None], hot & (rank == 1)[:, None]], axis=1)
    picks = picks.reshape(count, 256).astype(jnp.bfloat16)
    table = jnp.dot(fields, picks, preferred_element_type=jnp.float32)
    table = table.reshape(8, 2, 128)
    li, lj = table[0].astype(jnp.int32), table[1].astype(jnp.int32)
    first = lambda v: (v % 2) * 48 + (v // 2) * 3
    words = jnp.concatenate([first(li), first(lj), li, lj])
    scales = jnp.pad(table[2] + table[3] + table[4], ((0, 6), (0, 0)))
    return words, scales, source, rank


def meet_kernel(lq, rq, words_ref, scales_ref, trans_ref, lg, rg, rel_l, rel_r, got_ref, dr_ref,
                tf_ref, u_ref, w_ref, p_ref, pr_ref, q_ref, qr_ref, dl_ref, lhs_ref, out_ref, blk_ref, wv_ref, sv_ref, wt_ref, sc_ref,
                send, recv, osend, orecv, wsend, wrecv, ssend, srecv, loc):
    z, y, x, c = (lax.axis_index(n) for n in AXES)

    def dev(dz=0, dy=0, dx=0, dc=0):
        return (lax.rem(z + dz, 4), lax.rem(y + dy, 4), lax.rem(x + dx, 4), lax.rem(c + dc, 2))

    def plane(o):
        return dev(dy=lax.rem(o // 4, 4), dx=lax.rem(o, 4), dc=o // 16)

    def mirror(o):
        return (o // 16) * 16 + lax.rem(4 - lax.rem(o // 4, 4), 4) * 4 + lax.rem(4 - lax.rem(o, 4), 4)

    def remote(src, dst, a, b, to):
        return pltpu.make_async_remote_copy(
            src_ref=src, dst_ref=dst, send_sem=a, recv_sem=b, device_id=to, device_id_type=MESH)

    def out_copy(o):
        return remote(out_ref.at[o], got_ref.at[mirror(o)], osend.at[o], orecv.at[o], plane(o))

    def word_copy(o):
        return remote(words_ref, wv_ref.at[mirror(o)], wsend.at[o], wrecv.at[o], plane(o))

    def scale_copy(o):
        return remote(scales_ref, sv_ref.at[mirror(o)], ssend.at[o], srecv.at[o], plane(o))

    barrier = pltpu.get_barrier_semaphore()
    for o in range(1, 32):
        pl.semaphore_signal(barrier, inc=1, device_id=plane(jnp.int32(o)), device_id_type=MESH)
    for d in (1, 3):
        pl.semaphore_signal(barrier, inc=1, device_id=dev(dz=d), device_id_type=MESH)
    pl.semaphore_wait(barrier, 33)

    copies = {}

    def send_to(name, src, dst, to):
        i = len(copies)
        copy = remote(src, dst, send.at[i], recv.at[i], to)
        copy.start()
        copies[name] = copy

    got = lambda *names: [copies[n].wait_recv() for n in names]
    part = lambda d: lax.rem(x + d, 4)
    lo, hi = pl.ds(0, HALF), pl.ds(HALF, ROWS - HALF)
    lat = lambda dz, dx: ORDER[dx] * 4 + ORDER[dz]
    rat = lambda dc, dy, dx: dc * 16 + dy * 4 + dx

    def ring_l(dx):
        src = lq.at[x] if dx == 0 else lg.at[lat(0, dx)]
        send_to(("z+", dx), src, lg.at[lat(3, dx)], dev(dz=1))
        send_to(("z-", dx), src, lg.at[lat(1, dx)], dev(dz=3))

    def ring_r(dx):
        src = rq.at[x] if dx == 0 else rg.at[rat(0, 0, dx)]
        send_to(("y+", dx), src, rg.at[rat(0, 3, dx)], dev(dy=1))
        send_to(("y-", dx), src, rg.at[rat(0, 1, dx)], dev(dy=3))
        send_to(("c", 0, dx), src, rg.at[rat(1, 0, dx)], dev(dc=1))

    def relay(dl, dr):
        got(("z+", dl))
        send_to(("zr+", dl), lg.at[lat(3, dl), lo], lg.at[lat(2, dl), lo], dev(dz=1))
        got(("z-", dl))
        send_to(("zr-", dl), lg.at[lat(1, dl), hi], lg.at[lat(2, dl), hi], dev(dz=3))
        got(("y+", dr))
        send_to(("yr+", dr), rg.at[rat(0, 3, dr), lo], rg.at[rat(0, 2, dr), lo], dev(dy=1))
        send_to(("c", 3, dr), rg.at[rat(0, 3, dr)], rg.at[rat(1, 3, dr)], dev(dc=1))
        got(("y-", dr))
        send_to(("yr-", dr), rg.at[rat(0, 1, dr), hi], rg.at[rat(0, 2, dr), hi], dev(dy=3))
        send_to(("c", 1, dr), rg.at[rat(0, 1, dr)], rg.at[rat(1, 1, dr)], dev(dc=1))

    def last(dl, dr):
        got(("yr+", dr), ("yr-", dr))
        send_to(("c", 2, dr), rg.at[rat(0, 2, dr)], rg.at[rat(1, 2, dr)], dev(dc=1))
        got(("zr+", dl), ("zr-", dl))

    def product(src, weight, store, rest):
        lane = lax.broadcasted_iota(jnp.int32, (48, 128), 1)
        for e in range(2):
            own = (lane < 64) if e == 0 else (lane >= 64)
            lhs_ref[e * 832:e * 832 + 768, :128] = src[e * 768:(e + 1) * 768, :]
            for p in range(16):
                tail = (lane // 8) == (p % 8 + (8 if e == 0 else 0))
                x2 = src[PAIRED + 48 * p:PAIRED + 48 * p + 48, :]
                x3 = src[TAIL + 48 * (p // 8):TAIL + 48 * (p // 8) + 48, :]
                at = e * 832 + 48 * p
                lhs_ref[at:at + 48, 128:] = jnp.where(own, x2, jnp.where(tail, x3, jnp.zeros_like(x3)))
        for h in range(2):
            lhs_ref[768:832, 128 * h:128 * h + 128] = src[REM + 64 * h:REM + 64 * h + 64, :]
        first = jnp.dot(lhs_ref[:832, :], weight[0], preferred_element_type=jnp.float32)
        store(0, first[:768].reshape(48, 16, K))
        rest(first[768:])
        second = jnp.dot(lhs_ref[832:, :], weight[1], preferred_element_type=jnp.float32)
        store(48, second.reshape(48, 16, K))

    def load(src, k):
        return pltpu.make_async_copy(src, blk_ref.at[k], loc.at[k])

    def diagonal(main, rem, out, base, q, add):
        rows = tf_ref[pl.ds(pl.multiple_of(base + 48 * q, 8), 48), :]

        @pl.loop(0, 8)
        def _(t):
            for i in range(4):
                f = 4 * t + i
                group = (i % 2) * 48 + (2 * t + i // 2) * 3
                prod = main[pl.ds(group, 3)].reshape(48, K) * rows
                total = jnp.sum(prod, axis=0, keepdims=True)
                for r in range(2):
                    total += rem[pl.ds(2 * f + r, 1), :] * tf_ref[pl.ds(base + 192 + 2 * q + r, 1), :]
                if add:
                    total += out[pl.ds(f, 1), :]
                out[pl.ds(f, 1), :] = total

    def trailing():
        dr_ref[...] = jnp.zeros_like(dr_ref)

        @pl.loop(0, 4)
        def _(q):
            load(rq.at[q], 0).start()
            load(rq.at[q], 0).wait()

            def store(g, value):
                q_ref[g:g + 48] = value

            def rest(value):
                qr_ref[...] = value

            product(blk_ref.at[0], w_ref, store, rest)
            diagonal(q_ref, qr_ref, dr_ref, 200, q, True)

    def left(start, stop):
        load(lg.at[start], 0).start()

        @pl.loop(start, stop)
        def _(at):
            k = lax.rem(at - start, 2)

            @pl.when(at + 1 < stop)
            def _():
                load(lg.at[at + 1], 1 - k).start()

            load(lg.at[at], k).wait()

            def store(g, value):
                p_ref[at, g:g + 48] = value

            def rest(value):
                pr_ref[at] = value

            product(blk_ref.at[k], u_ref, store, rest)

            diagonal(p_ref.at[at], pr_ref.at[at], dl_ref.at[at], 0, x, False)

    send_to(("xl", 3), lq.at[part(1)], lg.at[lat(0, 3)], dev(dx=1))
    send_to(("xr", 1), rq.at[part(3)], rg.at[rat(0, 0, 1)], dev(dx=3))
    ring_l(0)
    ring_r(0)
    send_to(("xr", 3), rq.at[part(1)], rg.at[rat(0, 0, 3)], dev(dx=1))
    send_to(("xl", 1), lq.at[part(3)], lg.at[lat(0, 1)], dev(dx=3))
    send_to("l_rel", lq.at[part(2)], rel_l, dev(dx=1))
    send_to("r_rel", rq.at[part(2)], rel_r, dev(dx=3))

    @pl.loop(1, 32)
    def _(o):
        word_copy(o).start()
        scale_copy(o).start()

    wv_ref[0] = words_ref[...]
    sv_ref[0] = scales_ref[...]
    tf_ref[...] = jnp.zeros_like(tf_ref)
    tf_ref[:, :400] = trans_ref[...].astype(jnp.float32)
    for base, ref in ((0, u_ref), (200, w_ref)):
        tile = jnp.concatenate([tf_ref[base + 192:base + 200, :]] * 8).astype(jnp.bfloat16)
        half = tf_ref[base + 128:base + 192, :].astype(jnp.bfloat16)
        for e in range(2):
            ref[e, :128, :] = tf_ref[base:base + 128, :].astype(jnp.bfloat16)
            ref[e, 128 + 64 * e:192 + 64 * e, :] = half
            ref[e, 192 - 64 * e:256 - 64 * e, :] = tile
    for k, (src, dst) in enumerate([(lq, lg.at[lat(0, 0)]), (rq, rg.at[0])]):
        load(src.at[x], k).start()
        load(src.at[x], k).wait()
        out = pltpu.make_async_copy(blk_ref.at[k], dst, loc.at[2])
        out.start()
        out.wait()
    trailing()
    relay(0, 0)
    got(("xl", 3))
    ring_l(3)
    got(("xr", 1))
    ring_r(1)
    left(0, 2)
    last(0, 0)
    got(("xl", 1))
    ring_l(1)
    got(("xr", 3))
    ring_r(3)
    left(2, 4)
    relay(3, 1)
    left(4, 6)
    got("l_rel")
    send_to(("xl", 2), rel_l, lg.at[lat(0, 2)], dev(dx=1))
    got("r_rel")
    send_to(("xr", 2), rel_r, rg.at[rat(0, 0, 2)], dev(dx=3))
    last(3, 1)
    left(6, 9)
    relay(1, 3)
    got(("xl", 2))
    ring_l(2)
    got(("xr", 2))
    ring_r(2)
    left(9, 11)
    last(1, 3)
    left(11, 13)
    relay(2, 2)
    left(13, 15)
    last(2, 2)
    left(15, 16)
    for dx in range(4):
        for dy in range(4):
            copies[("c", dy, dx)].wait_recv()

    @pl.loop(1, 32)
    def _(o):
        word_copy(o).wait_recv()
        scale_copy(o).wait_recv()

    load(rg.at[31], 1).start()
    to_s = [pltpu.make_async_copy(wv_ref, wt_ref, loc.at[2]), pltpu.make_async_copy(sv_ref, sc_ref, loc.at[3])]
    for t in to_s:
        t.start()
    for t in to_s:
        t.wait()

    @pl.loop(0, 32)
    def _(step):
        o = 31 - step
        k = lax.rem(o, 2)

        @pl.when(o > 0)
        def _():
            load(rg.at[o - 1], 1 - k).start()

        load(rg.at[o], k).wait()

        def store(g, value):
            q_ref[g:g + 48] = value

        def rest(value):
            qr_ref[...] = value

        product(blk_ref.at[k], w_ref, store, rest)

        @pl.loop(0, 8)
        def _(t):
            for i in range(4):
                zs, xs, r = t // 2, lax.rem(t, 2) * 2 + i // 2, i % 2
                lane = ((zs * 4 + y) * 4 + xs) * 2 + c
                gi, gj, li, lj = (wt_ref[o, 2 * m + r, lane] for m in range(4))
                dz, dx = lax.rem(zs - z + 4, 4), lax.rem(xs - x + 4, 4)
                s = (lax.rem(dx, 3) + 1) * ((dx + 3) // 4) * 4 + (lax.rem(dz, 3) + 1) * ((dz + 3) // 4)
                prod = p_ref[s, pl.ds(gi, 3)] * q_ref[pl.ds(gj, 3)]
                total = jnp.sum(prod.reshape(48, K), axis=0, keepdims=True)
                for m in range(2):
                    total += pr_ref[s, pl.ds(2 * li + m, 1), :] * qr_ref[pl.ds(2 * lj + m, 1), :]
                out_ref[o, pl.ds(4 * t + i, 1), :] = total * sc_ref[o, r, lane] + dl_ref[s, pl.ds(li, 1), :]

        @pl.when(o > 0)
        def _():
            out_copy(o).start()

    own = pltpu.make_async_copy(out_ref.at[0], got_ref.at[0], loc.at[2])
    own.start()
    own.wait()
    for copy in copies.values():
        copy.wait_send()
    assert len(copies) == NCOPY

    @pl.loop(1, 32)
    def _(o):
        word_copy(o).wait_send()
        scale_copy(o).wait_send()
        out_copy(o).wait_recv()
        out_copy(o).wait_send()


def meet(lq, rq, words, scales, transform):
    blk = (ROWS, 128)
    any_ = pl.BlockSpec(memory_space=pl.ANY)
    vmem = pl.BlockSpec(memory_space=pltpu.VMEM)
    bf, f32 = jnp.bfloat16, jnp.float32
    dma = lambda n: pltpu.SemaphoreType.DMA((n,))
    out = jax.ShapeDtypeStruct
    return pl.pallas_call(
        meet_kernel,
        out_shape=(out((16,) + blk, bf), out((32,) + blk, bf), out(blk, bf), out(blk, bf), out((32, 32, K), f32),
                   out((32, K), f32)),
        in_specs=[any_, any_] + [vmem] * 3,
        out_specs=(any_,) * 5 + (vmem,),
        scratch_shapes=[
            pltpu.VMEM((400, K), f32), pltpu.VMEM((2, 256, K), bf), pltpu.VMEM((2, 256, K), bf),
            pltpu.VMEM((16, 96, 16, K), f32), pltpu.VMEM((16, 64, K), f32),
            pltpu.VMEM((96, 16, K), f32), pltpu.VMEM((64, K), f32),
            pltpu.VMEM((16, 32, K), f32), pltpu.VMEM((1600, 256), bf),
            pltpu.VMEM((32, 32, K), f32), pltpu.VMEM((2,) + blk, bf),
            pltpu.VMEM((32, 8, 128), jnp.int32), pltpu.VMEM((32, 8, 128), f32),
            pltpu.SMEM((32, 8, 128), jnp.int32), pltpu.SMEM((32, 8, 128), f32),
            dma(NCOPY), dma(NCOPY), dma(32), dma(32), dma(32), dma(32), dma(32), dma(32), dma(4),
        ],
        compiler_params=pltpu.CompilerParams(collective_id=0, has_side_effects=True, vmem_limit_bytes=67043328),
        name="meet",
    )(lq, rq, words, scales, transform)[4:]


def finish_kernel(where, got_ref, dr_ref, en_ref, sum_ref, part_ref, inbox_ref, send, recv):
    z, y, x, c = (lax.axis_index(n) for n in AXES)

    def dev(dz=0, dy=0, dx=0, dc=0):
        return (lax.rem(z + dz, 4), lax.rem(y + dy, 4), lax.rem(x + dx, 4), lax.rem(c + dc, 2))

    barrier = pltpu.get_barrier_semaphore()
    partners = [dev(**{k: d}) for k in ("dx", "dy", "dz") for d in (1, 2, 3)] + [dev(dc=1)]
    for p in partners:
        pl.semaphore_signal(barrier, inc=1, device_id=p, device_id_type=MESH)
    pl.semaphore_wait(barrier, len(partners))
    copies = []

    def send_to(src, dst, to):
        i = len(copies)
        copy = pltpu.make_async_remote_copy(
            src_ref=src, dst_ref=dst, send_sem=send.at[i], recv_sem=recv.at[i],
            device_id=to, device_id_type=MESH)
        copy.start()
        copies.append(copy)
        return copy

    me = ((z * 4 + y) * 4 + x) * 2 + c

    @pl.loop(0, 16)
    def _(t):
        for i in range(8):
            d = 8 * t + i
            dc, dy, n, lj = where[0, d], where[1, d], where[2, d], where[3, d]
            row = dr_ref[pl.ds(lj, 1), :]
            for dx in range(4):
                row += got_ref[dc, dy, dx, pl.ds(n, 1), :]
            en_ref[pl.ds(d, 1), :] = row[:, :400]

    value = en_ref[...]
    mean = jnp.sum(value * value, axis=1, keepdims=True) * jnp.float32(1.0 / 400.0)
    index = (me * 128 + lax.broadcasted_iota(jnp.int32, (128, 1), 0)).astype(jnp.float32)
    total = jnp.sum((index + 1.0) * jnp.float32(1.0 / 16384.0) * mean, axis=0, keepdims=True)
    total = jnp.broadcast_to(total * jnp.float32(2.0 / 16384.0), (8, 128))
    stages = [[dict(dx=d) for d in (1, 2, 3)], [dict(dy=d) for d in (1, 2, 3)], [dict(dz=d) for d in (1, 2, 3)], [dict(dc=1)]]
    slot = 0
    for k, stage in enumerate(stages):
        part_ref[k] = total
        sent = []
        for j, to in enumerate(stage):
            sent.append((slot, send_to(part_ref.at[k], inbox_ref.at[slot], dev(**to))))
            slot += 1
        for at, copy in sent:
            copy.wait_recv()
        values = [total] + [inbox_ref[at] for at, _ in sent]
        if len(values) == 4:
            total = (values[0] + values[2]) + (values[1] + values[3])
        else:
            total = values[0] + values[1]
    sum_ref[...] = total
    for copy in copies:
        copy.wait_send()


def finish(where, parts, dr):
    n = 10
    vmem = pl.BlockSpec(memory_space=pltpu.VMEM)
    return pl.pallas_call(
        finish_kernel,
        out_shape=(jax.ShapeDtypeStruct((128, 400), jnp.float32), jax.ShapeDtypeStruct((8, 128), jnp.float32)),
        in_specs=[pl.BlockSpec(memory_space=pltpu.SMEM), vmem, vmem],
        out_specs=(vmem, vmem),
        scratch_shapes=[
            pltpu.VMEM((4, 8, 128), jnp.float32),
            pltpu.VMEM((10, 8, 128), jnp.float32), pltpu.SemaphoreType.DMA((n,)),
            pltpu.SemaphoreType.DMA((n,)),
        ],
        compiler_params=pltpu.CompilerParams(collective_id=1, has_side_effects=True, vmem_limit_bytes=32 << 20),
        name="finish",
    )(where, parts.reshape(2, 4, 4, 32, K), dr)


def local(potentials, dimers, coupling, transform):
    z, y, x, c = (lax.axis_index(n) for n in AXES)
    words, scales, source, rank = slot_table(dimers, coupling)
    lq, rq = pack(potentials)

    parts, dr = meet(lq, rq, words, scales, transform)
    zs, ys, xs, cs = source // 32, (source // 8) % 4, (source // 2) % 4, source % 2
    where = jnp.stack([(cs - c) % 2, (ys - y) % 4, (zs * 4 + xs) * 2 + rank, dimers[:, 1] % 32])
    energies, total = finish(where, parts, dr)
    return energies, total[0, :1]


def solution(mesh):
    split = Mesh(mesh.devices.reshape(4, 4, 4, mesh.shape["sub"]), AXES)
    return jax.shard_map(
        local,
        mesh=split,
        in_specs=(P(AXES, None, None), P(AXES, None), P(AXES), P()),
        out_specs=(P(AXES, None), P()),
        check_vma=False,
    )
```
